128 devices in a mesh: ctx: 32 (over x, y_lo, z), exp: 4 (over y_hi, core).
Axes of the slice: x: 4, y: 4 (y_hi: 2, y_lo: 2; y = y_hi * 2 + y_lo), z: 4, core: 2. Of those that a mesh axis runs over, the one named last changes fastest.
Arguments:
- residual: bfloat16 [4, 4096, 2048], P('exp', 'ctx'), may hold values from -6 to 6
- query_heads: bfloat16 [4, 4096, 2048], P('exp', 'ctx'), may hold values from -6.5 to 6.5
- key_heads: bfloat16 [4, 4096, 256], P('exp', 'ctx'), may hold values from -6 to 6
- value_heads: bfloat16 [4, 4096, 256], P('exp', 'ctx'), may hold values from -6 to 6
- norm_gain: float32 [2048], replicated, may hold values from 0.1 to 1.9
- chosen_experts: int32 [4, 4096, 8], P('exp', 'ctx'), may hold values from 0 to 127, all different within a row; in each aligned block of 128 rows (0 to 127, 128 to 255, ..., all dimensions but the last counted through in order) at most 9 rows name the same one
- route_weights: float32 [4, 4096, 8], P('exp', 'ctx'), may hold values from 0.05 to 1
- gate_weight: bfloat16 [128, 2048, 768], P(('ctx', 'exp')), may hold values from -0.125 to 0.125
- up_weight: bfloat16 [128, 2048, 768], P(('ctx', 'exp')), may hold values from -0.125 to 0.125
- down_weight: bfloat16 [128, 768, 2048], P(('ctx', 'exp')), may hold values from -0.21875 to 0.21875
- cotangent: bfloat16 [4, 4096, 2048], P('exp', 'ctx'), may hold values from -6 to 6
Outputs:
- layer_out: bfloat16 [4, 4096, 2048], P('exp', 'ctx')
- residual_gradient: bfloat16 [4, 4096, 2048], P('exp', 'ctx')
- query_gradient: bfloat16 [4, 4096, 2048], P('exp', 'ctx')
- key_gradient: bfloat16 [4, 4096, 256], P('exp', 'ctx')
- value_gradient: bfloat16 [4, 4096, 256], P('exp', 'ctx')
- route_gradient: float32 [4, 4096, 8], P('exp', 'ctx')
The draws below stay inside these ranges and needn't reach their ends.
Inputs may be any that keep to these rules, and one draw needn't show every extreme that they name: `chosen_experts`: among the rows of one device no expert is named by more than 9 rows, a bound that some block reaches; the 8 experts of a row differ.
All inputs are finite; a program needn't handle non-finite values.
Results may differ from the reference program's by a relative error of at most 0.025.
Values may be sent and summed in bfloat16 or wider, within the bound.
A program may use at most 192 MiB of HBM per device.

```python
import math
import jax
import jax.numpy as jnp
import numpy as np
from jax import lax

D = 2048
H = 16
KVH = 2
DH = 128
F = 768
TOPK = 8
TOK_DEV = 128
EXPERTS = 128
SEQ = 4096
SEQS = 4
CAP = 9


def draw_query_heads(key, part):
    drawn_base = jnp.clip(jax.random.normal(jax.random.fold_in(key, 11), (SEQS, SEQ, H * DH), jnp.float32), -6.0, 6.0)
    return drawn_base.astype(jnp.bfloat16)


def draw_key_heads(key, part):
    drawn_base = jnp.clip(jax.random.normal(jax.random.fold_in(key, 12), (SEQS, SEQ, KVH * DH), jnp.float32), -6.0, 6.0)
    return drawn_base.astype(jnp.bfloat16)


def steps_of(key, shape, split, least, high):
    def one(dim, shards_of):
        steps = jax.random.uniform(jax.random.fold_in(jax.random.fold_in(key, 6), dim), (shards_of,), jnp.float32, least / len(split), high / len(split))
        return jnp.repeat(jnp.exp(steps), shape[dim] // shards_of).reshape((-1,) + (1,) * (len(shape) - dim - 1))

    factor_of = one(*split[0])
    for cut in split[1:]:
        factor_of = factor_of * one(*cut)
    return factor_of


def routed_block(own_key, own, number, rows, number_of, top, limit, slope):
    sequence = jax.random.permutation(own_key, number_of)
    heavy_load, usual = portions_of(number_of, rows * top, limit, slope, True), portions_of(number_of, rows * top, limit, slope, False)
    places = jnp.arange(number_of)

    def named(lengths, rotation):
        used = int((lengths > 0).sum())
        fixed = max(1, used // 4)
        shifted = fixed + (places - fixed + rotation * (used - fixed)) % max(1, number_of - fixed)
        return jnp.zeros((number_of,), jnp.int32).at[sequence[jnp.where(places < fixed, places, shifted)]].set(jnp.asarray(lengths, jnp.int32))

    lengths = jnp.where(number % 4 == 0, named(heavy_load, number // 4), named(usual, number - number // 4 - 1))
    mixed = jax.random.permutation(jax.random.fold_in(own, 3), number_of)
    source_of, taker = mixed[0:number_of // 2 * 2:2], mixed[1:number_of // 2 * 2:2]
    margin = jnp.minimum(lengths[source_of] - 1, limit - lengths[taker]) // 2
    margin = jnp.where((source_of == sequence[0]) | (taker == sequence[0]) | (lengths[taker] == 0), 0, jnp.maximum(margin, 0))
    shifted = jax.random.randint(jax.random.fold_in(own, 4), (number_of // 2,), 0, 1 << 20) % (margin + 1)
    lengths = lengths.at[source_of].add(-shifted).at[taker].add(shifted)
    labels = jnp.searchsorted(jnp.cumsum(lengths), jnp.arange(rows * top), side="right").astype(jnp.int32)
    table = labels.reshape(top, rows).T
    table = table[jax.random.permutation(jax.random.fold_in(own, 1), rows)]
    rotation = jax.random.randint(jax.random.fold_in(own, 2), (rows, 1), 0, top)
    return jnp.take_along_axis(table, (jnp.arange(top)[None, :] + rotation) % top, axis=1)


def portions_of(count, total, limit, skew, full):
    portions = [(1 << 20) // math.isqrt(grade ** skew) + 1 for grade in range(1, count + 1)]
    largest = limit if full else min(limit, max(-(-total // count), total * portions[0] // sum(portions)))
    least = 1 if total - largest >= count - 1 else 0
    counts, rest = [largest] + [least] * (count - 1), total - largest - least * (count - 1)
    while rest > 0:
        candidates = [i for i in range(1, count) if counts[i] < largest] or [i for i in range(1, count) if counts[i] < limit]
        whole, left = sum([portions[i] for i in candidates]), rest
        for i in candidates:
            extra = min(limit - counts[i], max(1, left * portions[i] // whole), rest)
            counts[i] = counts[i] + extra
            rest = rest - extra
    return np.array(counts)


def gaussian(rng, dims, deviation, limit, split=(), kind=jnp.bfloat16):
    values = deviation * jax.random.normal(rng, dims, jnp.float32)
    if split:
        values = values * steps_of(rng, dims, split, -0.22, 0.18)
    return jnp.clip(values, -limit, limit).astype(kind)


def setup_inputs(seed: int = 0) -> dict:
    arg_keys = jax.random.split(jax.random.key(seed), 12)
    residual = gaussian(arg_keys[0], (SEQS, SEQ, D), 1.0, 6.0, ((0, 4), (1, 32)))
    query_heads = draw_query_heads(jax.random.fold_in(arg_keys[11], 71), 0)
    key_heads = draw_key_heads(jax.random.fold_in(arg_keys[11], 71), 0)
    value_heads = gaussian(arg_keys[3], (SEQS, SEQ, KVH * DH), 1.0, 6.0, ((0, 4), (1, 32)))
    norm_gain = jnp.clip(1.0 + 0.18 * jax.random.normal(arg_keys[4], (D,), jnp.float32), 0.1, 1.9)
    chosen_experts_keys = jax.random.split(jax.random.fold_in(arg_keys[5], 1), SEQS * SEQ // TOK_DEV)
    chosen_experts_turns = jax.random.permutation(jax.random.fold_in(arg_keys[5], 3), SEQS * SEQ // TOK_DEV)
    chosen_experts = jax.vmap(lambda own, number: routed_block(jax.random.fold_in(arg_keys[5], 2), own, number, TOK_DEV, EXPERTS, TOPK, CAP, 0))(chosen_experts_keys, chosen_experts_turns).reshape((SEQS, SEQ, TOPK))
    route_weights = jnp.clip(jnp.exp(math.log(1.0) - 2.9957323 * jax.random.uniform(arg_keys[6], (SEQS, SEQ, TOPK), jnp.float32) ** steps_of(arg_keys[6], (SEQS, SEQ, TOPK), ((0, 4), (1, 32)), -0.2, 0.2)), 0.05, 1.0)
    gate_weight = gaussian(arg_keys[7], (EXPERTS, D, F), D ** -0.5, 0.125, ((0, 128),))
    up_weight = gaussian(arg_keys[8], (EXPERTS, D, F), D ** -0.5, 0.125, ((0, 128),))
    down_weight = gaussian(arg_keys[9], (EXPERTS, F, D), F ** -0.5, 0.21875, ((0, 128),))
    cotangent = gaussian(arg_keys[10], (SEQS, SEQ, D), 1.0, 6.0, ((0, 4), (1, 32)))
    return {"residual": residual, "query_heads": query_heads, "key_heads": key_heads, "value_heads": value_heads, "norm_gain": norm_gain, "chosen_experts": chosen_experts, "route_weights": route_weights, "gate_weight": gate_weight, "up_weight": up_weight, "down_weight": down_weight, "cotangent": cotangent}


NEG = -1e+30
EPSILON = 1e-06

def to_bfloat(values):
    return lax.optimization_barrier(values.astype(jnp.bfloat16)).astype(jnp.float32)

def attend_forward(query_seq, key_seq, value_seq):
    score_scale = DH ** (-0.5)
    block_rows = min(512, SEQ)
    out_parts = []
    log_parts = []
    for begin_row in range(0, SEQ, block_rows):
        end_row = begin_row + block_rows
        scores = jnp.einsum('ikgd,jkd->kgij', query_seq[begin_row:end_row], key_seq[:end_row]) * score_scale
        allowed = jnp.arange(end_row)[None, :] <= jnp.arange(begin_row, end_row)[:, None]
        scores = jnp.where(allowed, scores, NEG)
        row_max = lax.optimization_barrier(jnp.max(scores, axis=-1, keepdims=True))
        weights = jnp.where(allowed, jnp.exp(scores - row_max), 0.0)
        row_sum = lax.optimization_barrier(jnp.sum(weights, axis=-1, keepdims=True))
        mixed_part = jnp.einsum('kgij,jkd->kgid', to_bfloat(weights), value_seq[:end_row]) / row_sum
        out_parts.append(mixed_part)
        log_parts.append((row_max + jnp.log(row_sum))[..., 0])
    attended = jnp.concatenate(out_parts, axis=2)
    attended = jnp.transpose(attended, (2, 0, 1, 3)).reshape(SEQ, H * DH).astype(jnp.bfloat16)
    return (attended, jnp.concatenate(log_parts, axis=2))

def attend_backward(query_seq, key_seq, value_seq, attended, grad_out, log_sum):
    score_scale = DH ** (-0.5)
    block_rows = min(512, SEQ)
    row_dot = jnp.einsum('ikgd,ikgd->kgi', grad_out, attended)
    key_grad = jnp.zeros((SEQ, KVH, DH), jnp.float32)
    value_grad = jnp.zeros((SEQ, KVH, DH), jnp.float32)
    query_parts = []
    for begin_row in range(0, SEQ, block_rows):
        end_row = begin_row + block_rows
        query_part = query_seq[begin_row:end_row]
        grad_part = grad_out[begin_row:end_row]
        scores = jnp.einsum('ikgd,jkd->kgij', query_part, key_seq[:end_row]) * score_scale
        allowed = jnp.arange(end_row)[None, :] <= jnp.arange(begin_row, end_row)[:, None]
        weights = jnp.where(allowed, jnp.exp(scores - log_sum[:, :, begin_row:end_row, None]), 0.0)
        value_grad = value_grad.at[:end_row].add(jnp.einsum('kgij,ikgd->jkd', to_bfloat(weights), grad_part))
        grad_weights = jnp.einsum('ikgd,jkd->kgij', grad_part, value_seq[:end_row])
        grad_scores = to_bfloat(weights * (grad_weights - row_dot[:, :, begin_row:end_row, None]))
        query_parts.append(jnp.einsum('kgij,jkd->ikgd', grad_scores, key_seq[:end_row]) * score_scale)
        key_grad = key_grad.at[:end_row].add(jnp.einsum('kgij,ikgd->jkd', grad_scores, query_part) * score_scale)
    query_grad = jnp.concatenate(query_parts, axis=0).reshape(SEQ, H * DH).astype(jnp.bfloat16)
    return (query_grad, key_grad.reshape(SEQ, KVH * DH).astype(jnp.bfloat16), value_grad.reshape(SEQ, KVH * DH).astype(jnp.bfloat16))

def reference(residual, query_heads, key_heads, value_heads, norm_gain, chosen_experts, route_weights, gate_weight, up_weight, down_weight, cotangent):
    group_size = H // KVH
    tokens_all = SEQS * SEQ
    hidden_list = []
    saved = []
    for seq_index in range(SEQS):
        query_seq = query_heads[seq_index].astype(jnp.float32).reshape(SEQ, KVH, group_size, DH)
        key_seq = key_heads[seq_index].astype(jnp.float32).reshape(SEQ, KVH, DH)
        value_seq = value_heads[seq_index].astype(jnp.float32).reshape(SEQ, KVH, DH)
        attended, log_sum = attend_forward(query_seq, key_seq, value_seq)
        saved.append((query_seq, key_seq, value_seq, attended, log_sum))
        hidden_list.append((residual[seq_index].astype(jnp.float32) + attended.astype(jnp.float32)).astype(jnp.bfloat16))
    hidden = jnp.concatenate(hidden_list, axis=0)
    hidden_float = hidden.astype(jnp.float32)
    inverse = lax.rsqrt(lax.optimization_barrier(jnp.mean(hidden_float * hidden_float, axis=-1, keepdims=True)) + EPSILON)
    normed = (hidden_float * inverse * norm_gain).astype(jnp.bfloat16)
    chosen_flat = chosen_experts.reshape(-1).astype(jnp.int32)
    share_raw = route_weights.reshape(tokens_all, TOPK)
    route_total = lax.optimization_barrier(jnp.sum(share_raw, axis=-1, keepdims=True))
    route_share = share_raw / route_total
    share_flat = route_share.reshape(-1)
    cot_float = cotangent.reshape(tokens_all, D).astype(jnp.float32)
    assignments = tokens_all * TOPK
    slots_each = EXPERTS * CAP
    onehot_hits = (chosen_flat[:, None] == jnp.arange(EXPERTS, dtype=jnp.int32)[None, :]).astype(jnp.int32)
    earlier = jnp.cumsum(onehot_hits, axis=0) - onehot_hits
    slot_index = lax.optimization_barrier(jnp.sum(earlier * onehot_hits, axis=1)).astype(jnp.int32)
    table = jnp.full((EXPERTS, slots_each), -1, jnp.int32).at[chosen_flat, slot_index].set(jnp.arange(assignments, dtype=jnp.int32))

    def expert_rows(slot_ids):
        is_filled = slot_ids >= 0
        assign = jnp.maximum(slot_ids, 0)
        token_ids = assign // TOPK
        row_inputs = jnp.where(is_filled[:, None], normed[token_ids], jnp.zeros((), jnp.bfloat16))
        return (is_filled, assign, token_ids, row_inputs)

    def expert_forward(carry, stacked):
        moe_sum, route_dot = carry
        slot_ids, gate_mat, up_mat, down_mat = stacked
        is_filled, assign, token_ids, row_inputs = expert_rows(slot_ids)
        gate_act = jnp.dot(row_inputs, gate_mat, preferred_element_type=jnp.float32)
        up_act = jnp.dot(row_inputs, up_mat, preferred_element_type=jnp.float32)
        activation = (jax.nn.silu(gate_act) * up_act).astype(jnp.bfloat16)
        produced = to_bfloat(jnp.dot(activation, down_mat, preferred_element_type=jnp.float32))
        produced = jnp.where(is_filled[:, None], produced, 0.0)
        moe_sum = moe_sum.at[token_ids].add(share_flat[assign][:, None] * produced)
        route_dot = route_dot.at[assign].add(lax.optimization_barrier(jnp.sum(produced * cot_float[token_ids], axis=-1)))
        return ((moe_sum, route_dot), None)

    def expert_backward(carry, stacked):
        slot_ids, gate_mat, up_mat, down_mat = stacked
        is_filled, assign, token_ids, row_inputs = expert_rows(slot_ids)
        gate_act = jnp.dot(row_inputs, gate_mat, preferred_element_type=jnp.float32)
        up_act = jnp.dot(row_inputs, up_mat, preferred_element_type=jnp.float32)
        out_cot = jnp.where(is_filled[:, None], share_flat[assign][:, None] * cot_float[token_ids], 0.0).astype(jnp.bfloat16)
        act_cot = jnp.dot(out_cot, down_mat.T, preferred_element_type=jnp.float32)
        sigma_gate = jax.nn.sigmoid(gate_act)
        gate_cot = (act_cot * up_act * sigma_gate * (1.0 + gate_act * (1.0 - sigma_gate))).astype(jnp.bfloat16)
        up_cot = (act_cot * gate_act * sigma_gate).astype(jnp.bfloat16)
        row_cot = to_bfloat(jnp.dot(gate_cot, gate_mat.T, preferred_element_type=jnp.float32) + jnp.dot(up_cot, up_mat.T, preferred_element_type=jnp.float32))
        carry = carry.at[token_ids].add(jnp.where(is_filled[:, None], row_cot, 0.0))
        return (carry, None)
    stacked_all = (table, gate_weight, up_weight, down_weight)
    (moe_sum, route_dot), unused = lax.scan(expert_forward, (jnp.zeros((tokens_all, D), jnp.float32), jnp.zeros((assignments,), jnp.float32)), stacked_all)
    layer_out = (hidden_float + moe_sum).astype(jnp.bfloat16)
    route_dot = route_dot.reshape(tokens_all, TOPK)
    route_gradient = (route_dot - lax.optimization_barrier(jnp.sum(route_share * route_dot, axis=-1, keepdims=True))) / route_total
    normed_cot, unused = lax.scan(expert_backward, jnp.zeros((tokens_all, D), jnp.float32), stacked_all)
    gained = norm_gain * normed_cot
    hidden_cot = inverse * gained - hidden_float * inverse ** 3 * lax.optimization_barrier(jnp.mean(hidden_float * gained, axis=-1, keepdims=True))
    residual_gradient = (cot_float + hidden_cot).astype(jnp.bfloat16)
    query_list, key_list, value_list = ([], [], [])
    for seq_index in range(SEQS):
        query_seq, key_seq, value_seq, attended, log_sum = saved[seq_index]
        grad_out = residual_gradient[seq_index * SEQ:(seq_index + 1) * SEQ].astype(jnp.float32).reshape(SEQ, KVH, group_size, DH)
        attended_float = attended.astype(jnp.float32).reshape(SEQ, KVH, group_size, DH)
        query_grad, key_grad, value_grad = attend_backward(query_seq, key_seq, value_seq, attended_float, grad_out, log_sum)
        query_list.append(query_grad)
        key_list.append(key_grad)
        value_list.append(value_grad)
    return (layer_out.reshape(SEQS, SEQ, D), residual_gradient.reshape(SEQS, SEQ, D), jnp.stack(query_list), jnp.stack(key_list), jnp.stack(value_list), route_gradient.reshape(SEQS, SEQ, TOPK))
```

```python
import functools
import math

import jax
import jax.numpy as jnp
from jax import lax
from jax.experimental import pallas as pl
from jax.experimental.pallas import tpu as pltpu
from jax.sharding import PartitionSpec as P

H = 16
KVH = 2
DH = 128
TOPK = 8
GROUP = H // KVH
GQ = GROUP * DH

NEG = -1e30
EPSILON = 1e-06
SCALE = DH ** (-0.5)
SCALE2 = SCALE * math.log2(math.e)
SLOTS = 8
EXTRA = 256
KEY_BLOCK = 256
VMEM_LIMIT = 60 * 1024 * 1024

HIGHEST = lax.Precision.HIGHEST
NN = (((1,), (0,)), ((), ()))
NT = (((1,), (1,)), ((), ()))


def iota(shape, dim):
    return lax.broadcasted_iota(jnp.int32, shape, dim)


def dot(a, b, dims=NN, precision=None):
    return lax.dot_general(a, b, dims, precision=precision, preferred_element_type=jnp.float32)


def call(kernel, out_shape, args, flops=0, **kwargs):
    moved = sum(math.prod(a.shape) * a.dtype.itemsize for a in args)
    leaves = out_shape if isinstance(out_shape, (tuple, list)) else (out_shape,)
    moved += sum(math.prod(a.shape) * a.dtype.itemsize for a in leaves)
    return pl.pallas_call(
        kernel,
        out_shape=out_shape,
        compiler_params=pltpu.CompilerParams(vmem_limit_bytes=VMEM_LIMIT),
        cost_estimate=pl.CostEstimate(flops=flops, bytes_accessed=moved, transcendentals=0),
        **kwargs,
    )(*args)


def shape(dims, dtype):
    return jax.ShapeDtypeStruct(dims, dtype)


def repeat_rows(experts):
    dims = (experts * SLOTS, experts)
    return lax.shift_right_logical(iota(dims, 0), 3) == iota(dims, 1)


def repeat_lanes(experts):
    dims = (experts, experts * SLOTS)
    return iota(dims, 0) == lax.shift_right_logical(iota(dims, 1), 3)


def one(mask):
    return jnp.where(mask, 1.0, 0.0)


def low(mask):
    return one(mask).astype(jnp.bfloat16)


def spread_rows(rows_ref, slot_by_expert, send_ref, share_by_expert=None):
    experts, tokens = slot_by_expert.shape
    width = rows_ref.shape[1]
    total = experts * SLOTS
    repeat = repeat_rows(experts)
    slot = dot(low(repeat), slot_by_expert.astype(jnp.bfloat16))
    place = jnp.bitwise_and(iota((total, tokens), 0), SLOTS - 1)
    first = slot == place.astype(jnp.float32)
    ninth = slot == float(SLOTS)
    if share_by_expert is not None:
        share = dot(one(repeat), share_by_expert, precision=HIGHEST)
        first_share = jnp.sum(jnp.where(first, share, 0.0), axis=1, keepdims=True)
        ninth_share = jnp.sum(jnp.where(ninth, share, 0.0), axis=1, keepdims=True)
    pick = low(first)
    for c in range(width // EXTRA):
        part = dot(pick, rows_ref[:, c * EXTRA : (c + 1) * EXTRA])
        if share_by_expert is not None:
            part = part * first_share
        send_ref[:, c * EXTRA : (c + 1) * EXTRA] = part.astype(jnp.bfloat16)
    fold = jnp.concatenate([low(ninth & (place == r)) for r in range(SLOTS)], axis=1)
    folded = jnp.concatenate(
        [rows_ref[:, r * EXTRA : (r + 1) * EXTRA] for r in range(SLOTS)], axis=0
    )
    part = dot(fold, folded)
    if share_by_expert is not None:
        part = part * ninth_share
    send_ref[:, width:] = part.astype(jnp.bfloat16)


def send_cot_kernel(chosen_ref, route_ref, cot_ref, send_ref, slot_ref, slot_t_ref, share_ref):
    tokens = chosen_ref.shape[0]
    experts = slot_ref.shape[1]
    chosen = chosen_ref[...]
    route = route_ref[...]
    share_raw = route / jnp.sum(route, axis=1, keepdims=True)
    lanes = iota((tokens, experts), 1)
    hit = jnp.zeros((tokens, experts), jnp.float32)
    share = jnp.zeros((tokens, experts), jnp.float32)
    for k in range(TOPK):
        match = chosen[:, k : k + 1] == lanes
        hit = jnp.where(match, 1.0, hit)
        share = jnp.where(match, share_raw[:, k : k + 1], share)
    earlier = low(iota((tokens, tokens), 1) < iota((tokens, tokens), 0))
    slot = jnp.where(hit > 0.0, dot(earlier, hit.astype(jnp.bfloat16)), -1.0)
    slot_t = slot.T
    slot_ref[...] = slot
    slot_t_ref[...] = slot_t
    share_ref[...] = share
    spread_rows(cot_ref, slot_t, send_ref, share.T)


def send_normed_kernel(residual_ref, attended_ref, gain_ref, slot_t_ref, send_ref, hidden_ref, normed_ref):
    hidden = (residual_ref[...].astype(jnp.float32) + attended_ref[...].astype(jnp.float32)).astype(
        jnp.bfloat16
    )
    hidden_ref[...] = hidden
    hidden_float = hidden.astype(jnp.float32)
    inverse = lax.rsqrt(jnp.mean(hidden_float * hidden_float, axis=1, keepdims=True) + EPSILON)
    normed_ref[...] = (hidden_float * inverse * gain_ref[...]).astype(jnp.bfloat16)
    spread_rows(normed_ref, slot_t_ref[...], send_ref)


def unfold_ninth(rows_ref, ninth_ref):
    sources, width = ninth_ref.shape
    dims = (sources, sources * SLOTS)
    own = iota(dims, 0) == lax.shift_right_logical(iota(dims, 1), 3)
    place = jnp.bitwise_and(iota(dims, 1), SLOTS - 1)
    for r in range(SLOTS):
        ninth_ref[:, r * EXTRA : (r + 1) * EXTRA] = dot(
            low(own & (place == r)), rows_ref[:, width:]
        ).astype(jnp.bfloat16)


def fold_ninth(ninth_ref, out_ref):
    sources, width = ninth_ref.shape
    dims = (sources * SLOTS, sources)
    own = lax.shift_right_logical(iota(dims, 0), 3) == iota(dims, 1)
    place = jnp.bitwise_and(iota(dims, 0), SLOTS - 1)
    fold = jnp.concatenate([low(own & (place == r)) for r in range(SLOTS)], axis=1)
    folded = jnp.concatenate(
        [ninth_ref[:, r * EXTRA : (r + 1) * EXTRA] for r in range(SLOTS)], axis=0
    )
    out_ref[:, width:] = dot(fold, folded).astype(jnp.bfloat16)


def expert_kernel(
    rows_ref,
    cot_ref,
    gate_ref,
    up_ref,
    down_ref,
    back_ref,
    act_ref,
    rows_ninth,
    cot_ninth,
    gate_cot,
    up_cot,
    back_ninth,
):
    main = rows_ref.shape[0]
    sources = rows_ninth.shape[0]
    width = rows_ninth.shape[1]
    units = gate_ref.shape[1]
    unfold_ninth(rows_ref, rows_ninth)
    unfold_ninth(cot_ref, cot_ninth)
    block = 256

    def hidden_step(n, carry):
        cols = pl.ds(pl.multiple_of(n * block, block), block)
        gate_mat = gate_ref[:, cols]
        up_mat = up_ref[:, cols]
        down_mat = down_ref[cols, :]
        for rows, rows_in, cot_in in (
            (pl.ds(0, main), rows_ref[:, :width], cot_ref[:, :width]),
            (pl.ds(main, sources), rows_ninth[...], cot_ninth[...]),
        ):
            gate_act = dot(rows_in, gate_mat)
            up_act = dot(rows_in, up_mat)
            act_cot = dot(cot_in, down_mat, NT)
            sigma = 1.0 / (1.0 + jnp.exp(-gate_act))
            act = gate_act * sigma
            act_ref[rows, cols] = (act * up_act).astype(jnp.bfloat16)
            gate_cot[rows, cols] = (
                act_cot * up_act * sigma * (1.0 + gate_act * (1.0 - sigma))
            ).astype(jnp.bfloat16)
            up_cot[rows, cols] = (act_cot * act).astype(jnp.bfloat16)
        return carry

    lax.fori_loop(0, units // block, hidden_step, 0)

    def back_step(n, carry):
        cols = pl.ds(pl.multiple_of(n * block, block), block)
        gate_mat = gate_ref[cols, :]
        up_mat = up_ref[cols, :]
        back_ref[:, cols] = (
            dot(gate_cot[:main, :], gate_mat, NT) + dot(up_cot[:main, :], up_mat, NT)
        ).astype(jnp.bfloat16)
        back_ninth[:, cols] = (
            dot(gate_cot[main:, :], gate_mat, NT) + dot(up_cot[main:, :], up_mat, NT)
        ).astype(jnp.bfloat16)
        return carry

    lax.fori_loop(0, width // block, back_step, 0)
    fold_ninth(back_ninth, back_ref)


def produce_kernel(act_ref, down_ref, out_ref, out_ninth):
    main = out_ref.shape[0]
    width = out_ninth.shape[1]
    block = 256

    def step(n, carry):
        cols = pl.ds(pl.multiple_of(n * block, block), block)
        down_mat = down_ref[:, cols]
        out_ref[:, cols] = dot(act_ref[:main, :], down_mat).astype(jnp.bfloat16)
        out_ninth[:, cols] = dot(act_ref[main:, :], down_mat).astype(jnp.bfloat16)
        return carry

    lax.fori_loop(0, width // block, step, 0)
    fold_ninth(out_ninth, out_ref)


def residual_kernel(back_ref, slot_ref, hidden_ref, cot_ref, gain_ref, out_ref, normed_cot):
    tokens, width = hidden_ref.shape
    experts = slot_ref.shape[1]
    slot = dot(slot_ref[...].astype(jnp.bfloat16), low(repeat_lanes(experts)))
    place = jnp.bitwise_and(iota((tokens, experts * SLOTS), 1), SLOTS - 1)
    first = low(slot == place.astype(jnp.float32))
    ninth = slot == float(SLOTS)
    for c in range(width // EXTRA):
        cols = slice(c * EXTRA, (c + 1) * EXTRA)
        normed_cot[:, cols] = dot(first, back_ref[:, cols]) + dot(
            low(ninth & (place == c)), back_ref[:, width:]
        )
    hidden = hidden_ref[...].astype(jnp.float32)
    inverse = lax.rsqrt(jnp.mean(hidden * hidden, axis=1, keepdims=True) + EPSILON)
    gained = gain_ref[...] * normed_cot[...]
    mean = jnp.mean(hidden * gained, axis=1, keepdims=True)
    out_ref[...] = (
        cot_ref[...].astype(jnp.float32)
        + inverse * gained
        - hidden * (inverse * inverse * inverse * mean)
    ).astype(jnp.bfloat16)


def output_kernel(
    ret_ref, slot_ref, share_ref, chosen_ref, route_ref, hidden_ref, cot_ref, out_ref, route_out_ref
):
    tokens, width = hidden_ref.shape
    experts = slot_ref.shape[1]
    total = experts * SLOTS
    repeat = repeat_lanes(experts)
    slot = dot(slot_ref[...].astype(jnp.bfloat16), low(repeat))
    share = dot(share_ref[...], one(repeat), precision=HIGHEST)
    place = jnp.bitwise_and(iota((tokens, total), 1), SLOTS - 1)
    first = slot == place.astype(jnp.float32)
    ninth = slot == float(SLOTS)
    share_high = share.astype(jnp.bfloat16).astype(jnp.float32)
    share_rest = share - share_high

    def mix(mask, rows):
        return dot(jnp.where(mask, share_high, 0.0).astype(jnp.bfloat16), rows) + dot(
            jnp.where(mask, share_rest, 0.0).astype(jnp.bfloat16), rows
        )

    ninth_dots = jnp.zeros((tokens, total), jnp.float32)
    for c in range(width // EXTRA):
        cols = slice(c * EXTRA, (c + 1) * EXTRA)
        moe = mix(first, ret_ref[:, cols]) + mix(ninth & (place == c), ret_ref[:, width:])
        out_ref[:, cols] = (hidden_ref[:, cols].astype(jnp.float32) + moe).astype(jnp.bfloat16)
        ninth_dots = jnp.where(
            place == c, dot(cot_ref[:, cols], ret_ref[:, width:], NT), ninth_dots
        )
    dots = dot(cot_ref[...], ret_ref[:, :width], NT)
    picked = jnp.where(first, dots, jnp.where(ninth, ninth_dots, 0.0))
    owner = lax.shift_right_logical(iota((tokens, total), 1), 3)
    chosen = chosen_ref[...]
    route = route_ref[...]
    route_total = jnp.sum(route, axis=1, keepdims=True)
    route_share = route / route_total
    lanes = iota((tokens, TOPK), 1)
    route_dot = jnp.zeros((tokens, TOPK), jnp.float32)
    for k in range(TOPK):
        column = jnp.sum(
            jnp.where(owner == chosen[:, k : k + 1], picked, 0.0), axis=1, keepdims=True
        )
        route_dot = jnp.where(lanes == k, column, route_dot)
    route_out_ref[...] = (
        route_dot - jnp.sum(route_share * route_dot, axis=1, keepdims=True)
    ) / route_total


def heads_of(ref):
    return [ref[:, h * DH : (h + 1) * DH] for h in range(GROUP)]


def allowed_keys(index, begin, tokens):
    dims = (KEY_BLOCK, GROUP * tokens)
    return begin + iota(dims, 0) <= index * tokens + jnp.bitwise_and(iota(dims, 1), tokens - 1)


def forward_kernel(index_ref, q_ref, kv_ref, out_ref, log_ref, q_t):
    tokens = q_ref.shape[0]
    index = index_ref[0]
    for h, part in enumerate(heads_of(q_ref)):
        q_t[:, h * tokens : (h + 1) * tokens] = part.T

    def visit(block, state, masked):
        run_max, run_sum, acc = state
        begin = pl.multiple_of(block * KEY_BLOCK, KEY_BLOCK)
        keys = kv_ref[pl.ds(begin, KEY_BLOCK), :DH]
        values = kv_ref[pl.ds(begin, KEY_BLOCK), DH:]
        scores = dot(keys, q_t[...])
        if masked:
            scores = jnp.where(allowed_keys(index, begin, tokens), scores, NEG)
        new_max = jnp.maximum(run_max, jnp.max(scores, axis=0, keepdims=True))
        weights = jnp.exp2(scores * SCALE2 - new_max * SCALE2)
        keep = jnp.exp2((run_max - new_max) * SCALE2)
        run_sum = run_sum * keep + jnp.sum(weights, axis=0, keepdims=True)
        acc = acc * keep + dot(values.T, weights.astype(jnp.bfloat16))
        return new_max, run_sum, acc

    state = (
        jnp.full((1, GROUP * tokens), NEG, jnp.float32),
        jnp.zeros((1, GROUP * tokens), jnp.float32),
        jnp.zeros((DH, GROUP * tokens), jnp.float32),
    )
    full = (index * tokens) // KEY_BLOCK
    state = lax.fori_loop(0, full, lambda b, s: visit(b, s, False), state)
    run_max, run_sum, acc = visit(full, state, True)
    acc = acc / run_sum
    for h in range(GROUP):
        out_ref[:, h * DH : (h + 1) * DH] = (
            acc[:, h * tokens : (h + 1) * tokens].T.astype(jnp.bfloat16)
        )
    log_ref[0] = run_max * SCALE2 + jnp.log2(run_sum)


def backward_kernel(
    index_ref, q_ref, kv_ref, grad_ref, attended_ref, log_ref, dq_ref, dkv_ref, q_s, q_t, g_s, g_t, dq_acc
):
    tokens = q_ref.shape[0]
    index = index_ref[0]
    dots = []
    for h in range(GROUP):
        rows = slice(h * tokens, (h + 1) * tokens)
        cols = slice(h * DH, (h + 1) * DH)
        q_s[rows, :] = q_ref[:, cols]
        g_s[rows, :] = grad_ref[:, cols]
        q_t[:, rows] = q_ref[:, cols].T
        grad_t = grad_ref[:, cols].T
        g_t[:, rows] = grad_t
        dots.append(
            jnp.sum(
                grad_t.astype(jnp.float32) * attended_ref[:, cols].T.astype(jnp.float32),
                axis=0,
                keepdims=True,
            )
        )
    row_dot = jnp.concatenate(dots, axis=1)
    log_sum = log_ref[0]
    dq_acc[...] = jnp.zeros_like(dq_acc)

    def visit(block, masked):
        begin = pl.multiple_of(block * KEY_BLOCK, KEY_BLOCK)
        keys = kv_ref[pl.ds(begin, KEY_BLOCK), :DH]
        values = kv_ref[pl.ds(begin, KEY_BLOCK), DH:]
        weights = jnp.exp2(dot(keys, q_t[...]) * SCALE2 - log_sum)
        if masked:
            weights = jnp.where(allowed_keys(index, begin, tokens), weights, 0.0)
        cot = (weights * (dot(values, g_t[...]) - row_dot)).astype(jnp.bfloat16)
        dkv_ref[pl.ds(begin, KEY_BLOCK), DH:] = dot(weights.astype(jnp.bfloat16), g_s[...]).astype(
            jnp.bfloat16
        )
        dkv_ref[pl.ds(begin, KEY_BLOCK), :DH] = (dot(cot, q_s[...]) * SCALE).astype(jnp.bfloat16)
        dq_acc[...] += dot(keys.T, cot)

    full = (index * tokens) // KEY_BLOCK

    def step(block, carry):
        visit(block, False)
        return carry

    lax.fori_loop(0, full, step, 0)
    visit(full, True)
    for h in range(GROUP):
        dq_ref[:, h * DH : (h + 1) * DH] = (
            (dq_acc[:, h * tokens : (h + 1) * tokens] * SCALE).T.astype(jnp.bfloat16)
        )


def attend_forward(index, query, kv):
    tokens, width = query.shape
    seq = kv.shape[0]
    return call(
        forward_kernel,
        (shape((tokens, width), jnp.bfloat16), shape((KVH, 1, GROUP * tokens), jnp.float32)),
        (index, query, kv),
        flops=4 * tokens * seq * width,
        grid_spec=pltpu.PrefetchScalarGridSpec(
            num_scalar_prefetch=1,
            grid=(KVH,),
            in_specs=[
                pl.BlockSpec((tokens, GQ), lambda g, i: (0, g)),
                pl.BlockSpec((seq, 2 * DH), lambda g, i: (0, g)),
            ],
            out_specs=[
                pl.BlockSpec((tokens, GQ), lambda g, i: (0, g)),
                pl.BlockSpec((1, 1, GROUP * tokens), lambda g, i: (g, 0, 0)),
            ],
            scratch_shapes=[pltpu.VMEM((DH, GROUP * tokens), jnp.bfloat16)],
        ),
    )


def attend_backward(index, query, kv, grad, attended, log_sum):
    tokens, width = query.shape
    seq = kv.shape[0]
    rows = pl.BlockSpec((tokens, GQ), lambda g, i: (0, g))
    pairs = pl.BlockSpec((seq, 2 * DH), lambda g, i: (0, g))
    return call(
        backward_kernel,
        (shape((tokens, width), jnp.bfloat16), shape((seq, KVH * 2 * DH), jnp.bfloat16)),
        (index, query, kv, grad, attended, log_sum),
        flops=10 * tokens * seq * width,
        grid_spec=pltpu.PrefetchScalarGridSpec(
            num_scalar_prefetch=1,
            grid=(KVH,),
            in_specs=[
                rows,
                pairs,
                rows,
                rows,
                pl.BlockSpec((1, 1, GROUP * tokens), lambda g, i: (g, 0, 0)),
            ],
            out_specs=[rows, pairs],
            scratch_shapes=[
                pltpu.VMEM((GROUP * tokens, DH), jnp.bfloat16),
                pltpu.VMEM((DH, GROUP * tokens), jnp.bfloat16),
                pltpu.VMEM((GROUP * tokens, DH), jnp.bfloat16),
                pltpu.VMEM((DH, GROUP * tokens), jnp.bfloat16),
                pltpu.VMEM((DH, GROUP * tokens), jnp.float32),
            ],
        ),
    )


def pair_heads(key_rows, value_rows):
    parts = []
    for g in range(KVH):
        parts += [key_rows[:, g * DH : (g + 1) * DH], value_rows[:, g * DH : (g + 1) * DH]]
    return jnp.concatenate(parts, axis=1)


def exchange(rows, axes):
    return lax.all_to_all(rows, axes, split_axis=0, concat_axis=0, tiled=True)


def per_device(
    residual,
    query_heads,
    key_heads,
    value_heads,
    norm_gain,
    chosen_experts,
    route_weights,
    gate_weight,
    up_weight,
    down_weight,
    cotangent,
):
    bf16, f32 = jnp.bfloat16, jnp.float32
    tokens, width = residual.shape[1:]
    ctx_count = lax.axis_size("ctx")
    experts = ctx_count * lax.axis_size("exp")
    seq = tokens * ctx_count
    ctx_index = lax.axis_index("ctx")
    index = ctx_index.reshape(1).astype(jnp.int32)
    slots = experts * SLOTS
    wide = width + EXTRA
    units = gate_weight.shape[2]
    residual, query, cot = residual[0], query_heads[0], cotangent[0]
    chosen, route = chosen_experts[0], route_weights[0]
    gain = norm_gain[None]
    gate_mat, up_mat, down_mat = gate_weight[0], up_weight[0], down_weight[0]

    def to_devices(rows):
        return exchange(rows.reshape(experts, SLOTS, wide), ("ctx", "exp")).reshape(slots, wide)

    pair = pair_heads(key_heads[0], value_heads[0])
    kv = exchange(jnp.broadcast_to(pair[None], (ctx_count,) + pair.shape), "ctx")
    kv = kv.reshape(seq, 2 * KVH * DH)

    send_cot, slot, slot_t, share = call(
        send_cot_kernel,
        (
            shape((slots, wide), bf16),
            shape((tokens, experts), f32),
            shape((experts, tokens), f32),
            shape((tokens, experts), f32),
        ),
        (chosen, route, cot),
        flops=2 * slots * tokens * width,
    )
    send_cot, kv = lax.optimization_barrier((send_cot, kv))
    cot_in = to_devices(send_cot)
    attended, log_sum = attend_forward(index, query, kv)
    send_normed, hidden, normed = call(
        send_normed_kernel,
        (shape((slots, wide), bf16), shape((tokens, width), bf16), shape((tokens, width), bf16)),
        (residual, attended, gain, slot_t),
        flops=2 * slots * tokens * width,
    )
    incoming = to_devices(send_normed)

    row_cot, activation = call(
        expert_kernel,
        (shape((slots, wide), bf16), shape((slots + experts, units), bf16)),
        (incoming, cot_in, gate_mat, up_mat, down_mat),
        flops=10 * (slots + experts) * width * units,
        scratch_shapes=[
            pltpu.VMEM((experts, width), bf16),
            pltpu.VMEM((experts, width), bf16),
            pltpu.VMEM((slots + experts, units), bf16),
            pltpu.VMEM((slots + experts, units), bf16),
            pltpu.VMEM((experts, width), bf16),
        ],
    )
    cot_back = to_devices(row_cot)
    produced = call(
        produce_kernel,
        shape((slots, wide), bf16),
        (activation, down_mat),
        flops=2 * (slots + experts) * width * units,
        scratch_shapes=[pltpu.VMEM((experts, width), bf16)],
    )
    produced, cot_back = lax.optimization_barrier((produced, cot_back))
    returned = to_devices(produced)
    residual_gradient = call(
        residual_kernel,
        shape((tokens, width), bf16),
        (cot_back, slot, hidden, cot, gain),
        flops=2 * slots * tokens * width,
        scratch_shapes=[pltpu.VMEM((tokens, width), f32)],
    )
    query_gradient, pair_terms = attend_backward(
        index, query, kv, residual_gradient, attended, log_sum
    )
    pair_terms = exchange(pair_terms.reshape(ctx_count, tokens, 2 * KVH * DH), "ctx")
    counted = (jnp.arange(ctx_count, dtype=jnp.int32) >= ctx_index)[:, None, None]
    pair_sum = jnp.sum(jnp.where(counted, pair_terms.astype(f32), 0.0), axis=0).astype(bf16)
    layer_out, route_gradient = call(
        output_kernel,
        (shape((tokens, width), bf16), shape((tokens, TOPK), f32)),
        (returned, slot, share, chosen, route, hidden, cot),
        flops=6 * slots * tokens * width,
    )
    halves = [pair_sum[:, n * DH : (n + 1) * DH] for n in range(2 * KVH)]
    key_gradient = jnp.concatenate(halves[0::2], axis=1)
    value_gradient = jnp.concatenate(halves[1::2], axis=1)
    return (
        layer_out[None],
        residual_gradient[None],
        query_gradient[None],
        key_gradient[None],
        value_gradient[None],
        route_gradient[None],
    )


def solution(mesh):
    rows = P("exp", "ctx", None)
    weights = P(("ctx", "exp"), None, None)
    in_specs = (rows, rows, rows, rows, P(), rows, rows, weights, weights, weights, rows)
    return jax.shard_map(
        per_device, mesh=mesh, in_specs=in_specs, out_specs=(rows,) * 6, check_vma=False
    )
```
